128 devices in a mesh: wide: 16 (over y_hi, z, core), narrow: 8 (over y_lo, x).
Axes of the slice: x: 4, y: 4 (y_hi: 2, y_lo: 2; y = y_hi * 2 + y_lo), z: 4, core: 2. Of those that a mesh axis runs over, the one named last changes fastest.
Arguments:
- inputs: bfloat16 [1, 4096, 4096], P(None, 'narrow', 'wide'), may hold values from -6 to 6
- out_cotangent: bfloat16 [1, 1, 4096, 14336], P(None, None, ('wide', 'narrow')), may hold values from -0.0014648438 to 0.0014648438
- sign_bits: int32 [1, 4096, 16384], P(None, 'wide', 'narrow'), may hold values 0 or 1
- row_pick: int32 [1, 8192], replicated, may hold values from 0 to 4095
- col_pick: int32 [1, 8192], replicated, may hold values from 0 to 16383
Outputs:
- sketch: float32 [1, 1, 8192], P(None, None, ('wide', 'narrow'))
The draws below stay inside these ranges and needn't reach their ends.
All inputs are finite; a program needn't handle non-finite values. No bound on the sum of `sign_bits` on one device may be relied on, other than what follows from the above.
Results may differ from the reference program's by a relative error of at most 0.0003.
Values may be sent and summed in bfloat16 or wider, within the bound.
A program may use at most 128 MiB of HBM per device.

```python
import jax
import jax.numpy as jnp
from jax import lax

D = 4096
FF = 14336
FFP = 16384
MATS = 1
EXAMPLES = 1
TOK = 4096
SKETCH = 8192


def place_ends(array, stream_key, smallest, high):
    dims = array.shape
    spot = [jax.random.randint(jax.random.fold_in(stream_key, axis), (), 0, dims[axis]) for axis in range(len(dims))]
    array = array.at[tuple(spot)].set(smallest)
    longest = dims.index(max(dims))
    spot[longest] = (spot[longest] + 1) % dims[longest]
    return array.at[tuple(spot)].set(high)


def levels(stream_key, extent, pieces, smallest, largest):
    def one(position, parts):
        heights = jax.random.uniform(jax.random.fold_in(jax.random.fold_in(stream_key, 6), position), (parts,), jnp.float32, smallest / len(pieces), largest / len(pieces))
        return jnp.repeat(jnp.exp(heights), extent[position] // parts).reshape((-1,) + (1,) * (len(extent) - position - 1))

    gain = one(*pieces[0])
    for cut in pieces[1:]:
        gain = gain * one(*cut)
    return gain


def bell_draw(own_key, dims, deviation, limit, shards=(), held_as=jnp.bfloat16):
    result = deviation * jax.random.normal(own_key, dims, jnp.float32)
    if shards:
        result = result * levels(own_key, dims, shards, -0.22, 0.18)
    return jnp.clip(result, -limit, limit).astype(held_as)


def setup_inputs(seed: int = 0) -> dict:
    streams_of = jax.random.split(jax.random.key(seed), 6)
    return {
        "inputs": bell_draw(streams_of[0], (EXAMPLES, TOK, D), 1.0, 6.0, ((1, 8), (2, 16))),
        "out_cotangent": bell_draw(streams_of[1], (MATS, EXAMPLES, TOK, FF), (1.0 / TOK), 0.0014648438, ((2, 128),)),
        "sign_bits": place_ends((jax.random.randint(streams_of[2], (MATS, D, FFP), 0, 2) < 1).astype(jnp.int32), jax.random.fold_in(streams_of[2], 1), 0, 1),
        "row_pick": place_ends(jax.random.randint(streams_of[3], (MATS, SKETCH), 0, D), jax.random.fold_in(streams_of[3], 1), 0, D - 1).astype(jnp.int32),
        "col_pick": place_ends(jax.random.randint(streams_of[4], (MATS, SKETCH), 0, FFP), jax.random.fold_in(streams_of[4], 1), 0, FFP - 1).astype(jnp.int32),
    }


def hadamard(length):
    index = jnp.arange(length, dtype=jnp.int32)
    parity = jnp.zeros((length, length), jnp.int32)
    for bit_number in range(length.bit_length() - 1):
        parity = parity ^ index[:, None] >> bit_number & 1 & (index[None, :] >> bit_number & 1)
    return (1 - 2 * parity).astype(jnp.float32)

def transform_last(block):
    width_all = block.shape[-1]
    leading = block.ndim - 1
    factors = []
    remain = width_all
    while remain > 1:
        factor = min(128, remain)
        factors.append(factor)
        remain = remain // factor
    shaped = block.reshape(block.shape[:-1] + tuple(factors))
    for placed, factor in enumerate(factors):
        mixed = jnp.tensordot(shaped, hadamard(factor), axes=([leading + placed], [0]), precision=lax.Precision.HIGHEST)
        shaped = jnp.moveaxis(mixed, -1, leading + placed)
    return shaped.reshape(block.shape)

def reference(inputs, out_cotangent, sign_bits, row_pick, col_pick):
    row_index = jnp.arange(D, dtype=jnp.int32)
    results = []
    for example in range(EXAMPLES):
        per_matrix = []
        for matrix in range(MATS):
            grad = jnp.dot(inputs[example].T, out_cotangent[matrix, example], preferred_element_type=jnp.float32)
            padded = jnp.pad(grad, ((0, 0), (0, FFP - FF)))
            padded = padded * (2 * sign_bits[matrix] - 1).astype(jnp.float32)
            columns_done = transform_last(padded)
            chosen = columns_done[:, col_pick[matrix]]
            parity = jnp.zeros((SKETCH, D), jnp.int32)
            for bit_number in range(D.bit_length() - 1):
                parity = parity ^ row_pick[matrix][:, None] >> bit_number & 1 & (row_index[None, :] >> bit_number & 1)
            row_signs = (1 - 2 * parity).astype(jnp.float32)
            values = lax.optimization_barrier(jnp.sum(row_signs * chosen.T, axis=1))
            per_matrix.append(values / jnp.sqrt(jnp.float32(SKETCH)))
        results.append(jnp.stack(per_matrix))
    return jnp.stack(results)
```

```python
import functools

import jax
import jax.numpy as jnp
from jax import lax
from jax.experimental import pallas as pl
from jax.experimental.pallas import tpu as pltpu
from jax.sharding import PartitionSpec as P

MESH = pl.DeviceIdType.MESH
F32 = jnp.float32
BF16 = jnp.bfloat16
I32 = jnp.int32
VMEM_LIMIT = 60 << 20

TOK = 32
COLS = 2048
ROWS = 256
LAST = 7


def place():
    wide = lax.axis_index("wide")
    narrow = lax.axis_index("narrow")
    return wide, narrow, wide // 8, (wide // 2) % 4, wide % 2, narrow // 4, narrow % 4


def device(y_hi, z, core, y_lo, x):
    return (y_hi * 8 + z * 2 + core, y_lo * 4 + x)


def remote(src, dst, send, recv, target):
    return pltpu.make_async_remote_copy(
        src_ref=src, dst_ref=dst, send_sem=send, recv_sem=recv, device_id=target, device_id_type=MESH
    )


def fold_parity(value, top):
    while top:
        value = value ^ (value >> top)
        top //= 2
    return value & 1


def hadamard(length):
    rows = lax.broadcasted_iota(I32, (length, length), 0)
    cols = lax.broadcasted_iota(I32, (length, length), 1)
    return (1 - 2 * fold_parity(rows & cols, 8)).astype(F32).astype(BF16)


def split(value):
    high = value.astype(BF16)
    return high, (value - high.astype(F32)).astype(BF16)


def grad_kernel(
    x_ref, cot_ref, bits_ref, out_ref,
    gbuf, xbuf, xt, bits, own_sign, far_sign,
    a_send, a_recv, y_send, y_recv, x_send, x_recv, s_send, s_recv,
    b_send, b_recv, r_send, r_recv, c_send, c_recv, local_sem,
):
    _, narrow, y_hi, z, core, y_lo, x = place()
    real = narrow != LAST

    def dev(y_hi=y_hi, z=z, core=core, y_lo=y_lo, x=x):
        return device(y_hi, z, core, y_lo, x)

    z_up, z_down, z_far = (z + 1) % 4, (z + 3) % 4, (z + 2) % 4
    barrier = pltpu.get_barrier_semaphore()
    peers = [dev(y_lo=(narrow ^ o) // 4, x=(narrow ^ o) % 4) for o in range(1, 8)]
    peers += [dev(y_hi=1 - y_hi), dev(y_hi=1 - y_hi, y_lo=1 - y_lo)]
    peers += [dev(z=z_up), dev(z=z_down), dev(core=1 - core)]
    for peer in peers:
        pl.semaphore_signal(barrier, inc=1, device_id=peer, device_id_type=MESH)

    bits_copy = pltpu.make_async_copy(bits_ref.at[0], bits, local_sem.at[0])
    bits_copy.start()

    def slot(z_at, core_at, offset):
        return pl.ds(pl.multiple_of(((z_at * 2 + core_at) * 8 + (narrow ^ offset)) * TOK, TOK), TOK)

    def columns(index):
        return pl.ds(pl.multiple_of(index * COLS, COLS), COLS)

    own_copy = pltpu.make_async_copy(
        cot_ref.at[0, 0, :, columns(narrow)], gbuf.at[slot(z, core, 0)], local_sem.at[1]
    )

    @pl.when(real)
    def _():
        own_copy.start()

    pl.semaphore_wait(barrier, len(peers))

    def y_copy(target_lo):
        rel = y_hi ^ y_lo
        return remote(
            x_ref.at[0], xbuf.at[x, rel], y_send.at[target_lo], y_recv.at[rel],
            dev(y_hi=y_lo, y_lo=target_lo),
        )

    self_copy = pltpu.make_async_copy(x_ref.at[0], xbuf.at[x, 0], y_recv.at[0])
    for target_lo in range(2):
        mine = (y_hi == y_lo) & (y_lo == target_lo)

        @pl.when(mine)
        def _():
            self_copy.start()

        @pl.when(jnp.logical_not(mine))
        def _():
            y_copy(target_lo).start()

    def a_copy(offset):
        target = narrow ^ offset
        return remote(
            cot_ref.at[0, 0, :, columns(target)],
            gbuf.at[pl.ds(pl.multiple_of(((z * 2 + core) * 8 + narrow) * TOK, TOK), TOK)],
            a_send.at[offset], a_recv.at[offset],
            dev(y_lo=target // 4, x=target % 4),
        )

    for offset in range(1, 8):

        @pl.when((narrow ^ offset) != LAST)
        def _():
            a_copy(offset).start()

    bits_copy.wait()

    @pl.loop(0, ROWS // 16)
    def _(step):
        rows = pl.ds(pl.multiple_of(step * 16, 16), 16)
        own_sign[rows, :] = (2 * bits[rows, :] - 1).astype(F32).astype(BF16)

    def x_copy(rel, offset):
        return remote(
            xbuf.at[x, rel], xbuf.at[x, rel], x_send.at[rel, offset], x_recv.at[rel, offset],
            dev(x=x ^ offset),
        )

    for rel in range(2):
        if rel == 0:
            @pl.when(y_hi == y_lo)
            def _():
                self_copy.wait()

            @pl.when(y_hi != y_lo)
            def _():
                remote(x_ref.at[0], xbuf.at[x, 0], y_send.at[0], y_recv.at[0], dev(y_lo=1 - y_lo)).wait_recv()
        else:
            remote(x_ref.at[0], xbuf.at[x, 1], y_send.at[0], y_recv.at[1], dev(y_lo=1 - y_lo)).wait_recv()
        for offset in (1, 3, 2):
            x_copy(rel, offset).start()

    sign_copy = remote(own_sign, far_sign, s_send.at[0], s_recv.at[0], dev(y_hi=1 - y_hi))

    def ring_copy(direction, offset):
        rows = gbuf.at[slot(z, core, offset)]
        return remote(
            rows, rows, b_send.at[direction, offset], b_recv.at[direction, offset],
            dev(z=z_up if direction == 0 else z_down),
        )

    def relay_copy(direction, offset):
        source = z_down if direction == 0 else z_up
        base = ((source * 2 + core) * 8 + (narrow ^ offset)) * TOK + direction * (TOK // 2)
        rows = gbuf.at[pl.ds(pl.multiple_of(base, TOK // 2), TOK // 2)]
        return remote(
            rows, rows, r_send.at[direction, offset], r_recv.at[direction, offset],
            dev(z=z_up if direction == 0 else z_down),
        )

    z_of = (z, z_down, z_far, z_up)

    def core_copy(distance, offset):
        rows = gbuf.at[slot(z_of[distance], core, offset)]
        return remote(
            rows, rows, c_send.at[distance, offset], c_recv.at[distance, offset], dev(core=1 - core)
        )

    def multiply(distance, first, last):
        z_at = z_of[distance]

        @pl.when(x != z_at)
        def _():
            for rel in range(2):
                x_off = x ^ z_at
                remote(
                    xbuf.at[z_at, rel], xbuf.at[z_at, rel], x_send.at[rel, 1], x_recv.at[rel, x_off], dev(x=z_at)
                ).wait_recv()

        for offset in range(8):
            core_copy(distance, offset).wait_recv()
        for rel in range(2):
            xt[rel * ROWS:(rel + 1) * ROWS, :] = xbuf[z_at, rel].T
        tokens = pl.ds(pl.multiple_of(z_at * 512, 512), 512)

        @pl.loop(0, COLS // 256)
        def _(tile):
            cols = pl.ds(pl.multiple_of(tile * 256, 256), 256)
            part = jnp.dot(xt[...], gbuf[tokens, cols], preferred_element_type=F32)
            for rel, sign in ((0, own_sign), (1, far_sign)):
                value = part[rel * ROWS:(rel + 1) * ROWS]
                if not first:
                    value = value + out_ref[rel, :, cols]
                if last:
                    value = value * sign[:, cols].astype(F32)
                out_ref[rel, :, cols] = value

    @pl.when(real)
    def _():
        sign_copy.start()
        for offset in range(8):
            if offset == 0:
                own_copy.wait()
            else:
                remote(
                    cot_ref.at[0, 0, :, columns(narrow)], gbuf.at[slot(z, core, offset)],
                    a_send.at[offset], a_recv.at[offset], dev(core=1 - core),
                ).wait_recv()
            ring_copy(0, offset).start()
            ring_copy(1, offset).start()
            core_copy(0, offset).start()
        for offset in range(8):
            for direction in range(2):
                rows = gbuf.at[slot(z_down if direction == 0 else z_up, core, offset)]
                remote(
                    rows, rows, b_send.at[direction, offset], b_recv.at[direction, offset], dev(z=z_up)
                ).wait_recv()
                relay_copy(direction, offset).start()
                core_copy(1 if direction == 0 else 3, offset).start()
        multiply(0, True, False)
        multiply(1, False, False)
        multiply(3, False, False)
        for offset in range(8):
            for direction in range(2):
                base = ((z_far * 2 + core) * 8 + (narrow ^ offset)) * TOK + direction * (TOK // 2)
                rows = gbuf.at[pl.ds(pl.multiple_of(base, TOK // 2), TOK // 2)]
                remote(
                    rows, rows, r_send.at[direction, offset], r_recv.at[direction, offset], dev(z=z_up)
                ).wait_recv()
            core_copy(2, offset).start()
        sign_copy.wait_recv()
        multiply(2, False, True)
        sign_copy.wait_send()
        for offset in range(8):
            for direction in range(2):
                ring_copy(direction, offset).wait_send()
                relay_copy(direction, offset).wait_send()
            for distance in range(4):
                core_copy(distance, offset).wait_send()

    @pl.when(jnp.logical_not(real))
    def _():
        out_ref[...] = jnp.zeros_like(out_ref)
        for offset in range(1, 4):
            for rel in range(2):
                remote(
                    xbuf.at[x ^ offset, rel], xbuf.at[x ^ offset, rel], x_send.at[rel, 1], x_recv.at[rel, offset],
                    dev(x=x ^ offset),
                ).wait_recv()

    for rel in range(2):
        for offset in (1, 3, 2):
            x_copy(rel, offset).wait_send()
    for target_lo in range(2):
        mine = (y_hi == y_lo) & (y_lo == target_lo)

        @pl.when(jnp.logical_not(mine))
        def _():
            y_copy(target_lo).wait_send()

    for offset in range(1, 8):

        @pl.when((narrow ^ offset) != LAST)
        def _():
            a_copy(offset).wait_send()


def gradient(inputs, out_cotangent, sign_bits):
    any_spec = pl.BlockSpec(memory_space=pl.ANY)
    dma = pltpu.SemaphoreType.DMA
    return pl.pallas_call(
        grad_kernel,
        out_shape=jax.ShapeDtypeStruct((2, ROWS, COLS), F32),
        in_specs=[any_spec] * 3,
        out_specs=pl.BlockSpec(memory_space=pltpu.VMEM),
        scratch_shapes=[
            pltpu.VMEM((2048, COLS), BF16),
            pltpu.VMEM((4, 2, 512, ROWS), BF16),
            pltpu.VMEM((2 * ROWS, 512), BF16),
            pltpu.VMEM((ROWS, COLS), I32),
            pltpu.VMEM((ROWS, COLS), BF16),
            pltpu.VMEM((ROWS, COLS), BF16),
            dma((8,)), dma((8,)), dma((2,)), dma((2,)), dma((2, 4)), dma((2, 4)), dma((1,)), dma((1,)),
            dma((2, 8)), dma((2, 8)), dma((2, 8)), dma((2, 8)), dma((4, 8)), dma((4, 8)), dma((2,)),
        ],
        compiler_params=pltpu.CompilerParams(
            collective_id=0, has_side_effects=True, vmem_limit_bytes=VMEM_LIMIT
        ),
    )(inputs, out_cotangent, sign_bits)


def sample_kernel(index_ref, grad_ref, sign_ref, scale_ref, out_ref, table, rows):
    mix = hadamard(ROWS)
    for tile in range(8):
        done = []
        for rel in range(2):
            high, low = split(grad_ref[rel, :, 256 * tile:256 * (tile + 1)])
            done.append(jnp.dot(mix, high, preferred_element_type=F32) + jnp.dot(mix, low, preferred_element_type=F32))
        for rel, value in ((0, done[0] + done[1]), (1, done[0] - done[1])):
            left, right = value[:, :128], value[:, 128:]
            base = tile * 1024 + rel * ROWS
            table[base:base + ROWS, :] = left + right
            table[base + 512:base + 512 + ROWS, :] = left - right

    @pl.loop(0, 64)
    def _(step):
        start = pl.multiple_of(step * 8, 8)
        for half in range(2):
            value = [table[pl.ds((2 * tile + half) * 512 + start, 8), :] for tile in range(8)]
            for bit in (1, 2, 4):
                value = [
                    value[tile ^ bit] - value[tile] if tile & bit else value[tile] + value[tile | bit]
                    for tile in range(8)
                ]
            for tile in range(8):
                table[pl.ds((2 * tile + half) * 512 + start, 8), :] = value[tile]

    unroll = 32

    @pl.loop(0, 8192 // unroll)
    def _(step):
        base = pl.multiple_of(step * unroll, unroll)
        for i in range(unroll):
            rows[pl.ds(base + i, 1), :] = table[pl.ds(index_ref[base + i], 1), :]

    ones = jnp.ones((8, 128), BF16)
    last_dims = (((1,), (1,)), ((), ()))

    @pl.loop(0, 16)
    def _(step):
        span = pl.ds(pl.multiple_of(step * 512, 512), 512)
        high, low = split(rows[span, :] * sign_ref[span, :].astype(F32))
        total = lax.dot_general(ones, high, last_dims, preferred_element_type=F32)
        total = total + lax.dot_general(ones, low, last_dims, preferred_element_type=F32)
        for part in range(4):
            out_ref[step, part:part + 1, :] = total[0:1, part * 128:(part + 1) * 128] * scale_ref[step, part:part + 1, :]


def sample(index, grads, signs, scale):
    vmem = pl.BlockSpec(memory_space=pltpu.VMEM)
    return pl.pallas_call(
        sample_kernel,
        out_shape=jax.ShapeDtypeStruct((16, 4, 128), F32),
        in_specs=[pl.BlockSpec(memory_space=pltpu.SMEM), vmem, vmem, vmem],
        out_specs=vmem,
        scratch_shapes=[pltpu.VMEM((8192, 128), F32), pltpu.VMEM((8192, 128), F32)],
        compiler_params=pltpu.CompilerParams(vmem_limit_bytes=VMEM_LIMIT),
    )(index, grads, signs, scale)


def sum_kernel(term_ref, out_ref, first, partial, second, w_send, w_recv, n_send, n_recv):
    wide, narrow = lax.axis_index("wide"), lax.axis_index("narrow")
    barrier = pltpu.get_barrier_semaphore()
    for offset in range(1, 16):
        pl.semaphore_signal(barrier, inc=1, device_id=(wide ^ offset, narrow), device_id_type=MESH)
    for offset in range(1, 8):
        pl.semaphore_signal(barrier, inc=1, device_id=(wide, narrow ^ offset), device_id_type=MESH)
    pl.semaphore_wait(barrier, 22)

    def wide_copy(offset):
        return remote(
            term_ref.at[wide ^ offset], first.at[offset], w_send.at[offset], w_recv.at[offset], (wide ^ offset, narrow)
        )

    def narrow_copy(offset):
        target = narrow ^ offset
        return remote(
            partial.at[target // 2], second.at[offset], n_send.at[offset], n_recv.at[offset], (wide, target)
        )

    for offset in range(1, 16):
        wide_copy(offset).start()
    total = term_ref[wide]
    for offset in range(1, 16):
        wide_copy(offset).wait_recv()
        total = total + first[offset]
    for row in range(4):
        partial[row] = total[row:row + 1]
    for offset in range(1, 8):
        narrow_copy(offset).start()
    line = partial[narrow // 2]
    for offset in range(1, 8):
        narrow_copy(offset).wait_recv()
        line = line + second[offset]
    out_ref[0] = jnp.where(narrow % 2 == 1, line[:, 64:], line[:, :64])
    for offset in range(1, 16):
        wide_copy(offset).wait_send()
    for offset in range(1, 8):
        narrow_copy(offset).wait_send()


def sum_terms(terms):
    vmem = pl.BlockSpec(memory_space=pltpu.VMEM)
    dma = pltpu.SemaphoreType.DMA
    return pl.pallas_call(
        sum_kernel,
        out_shape=jax.ShapeDtypeStruct((1, 1, 64), F32),
        in_specs=[vmem],
        out_specs=vmem,
        scratch_shapes=[
            pltpu.VMEM((16, 4, 128), F32), pltpu.VMEM((4, 1, 128), F32), pltpu.VMEM((8, 1, 128), F32),
            dma((16,)), dma((16,)), dma((8,)), dma((8,)),
        ],
        compiler_params=pltpu.CompilerParams(
            collective_id=1, has_side_effects=True, vmem_limit_bytes=VMEM_LIMIT
        ),
    )(terms)


def body(inputs, out_cotangent, sign_bits, row_pick, col_pick):
    wide, narrow = lax.axis_index("wide"), lax.axis_index("narrow")
    row, col = row_pick[0], col_pick[0]
    index = (col // 128) % 16 * 512 + row // 2048 * 256 + row % 256
    parity = fold_parity((wide & (row // 256)) ^ (narrow & (col // 2048)), 8)
    scale = jnp.where(parity == 1, F32(-1.0), F32(1.0)) / jnp.sqrt(F32(row.shape[0]))
    lanes = jnp.arange(128, dtype=I32)
    signs = (1 - 2 * fold_parity((col % 128)[:, None] & lanes[None, :], 4)).astype(BF16)
    grads = gradient(inputs, out_cotangent, sign_bits)
    terms = sample(index, grads, signs, scale.reshape(16, 4, 128))
    return sum_terms(terms)


def solution(mesh):
    return jax.shard_map(
        body,
        mesh=mesh,
        in_specs=(
            P(None, "narrow", "wide"),
            P(None, None, ("wide", "narrow"), None),
            P(None, "wide", "narrow"),
            P(),
            P(),
        ),
        out_specs=P(None, None, ("wide", "narrow")),
        check_vma=False,
    )
```

```python
import functools

import jax
import jax.numpy as jnp
from jax import lax
from jax.experimental import pallas as pl
from jax.experimental.pallas import tpu as pltpu
from jax.sharding import PartitionSpec as P

MESH = pl.DeviceIdType.MESH
F32 = jnp.float32
BF16 = jnp.bfloat16
I32 = jnp.int32
VMEM_LIMIT = 60 << 20

TOK = 32
COLS = 2048
ROWS = 256
LAST = 7


def place():
    wide = lax.axis_index("wide")
    narrow = lax.axis_index("narrow")
    return wide, narrow, wide // 8, (wide // 2) % 4, wide % 2, narrow // 4, narrow % 4


def device(y_hi, z, core, y_lo, x):
    return (y_hi * 8 + z * 2 + core, y_lo * 4 + x)


def remote(src, dst, send, recv, target):
    return pltpu.make_async_remote_copy(
        src_ref=src, dst_ref=dst, send_sem=send, recv_sem=recv, device_id=target, device_id_type=MESH
    )


def fold_parity(value, top):
    while top:
        value = value ^ (value >> top)
        top //= 2
    return value & 1


def hadamard(length):
    rows = lax.broadcasted_iota(I32, (length, length), 0)
    cols = lax.broadcasted_iota(I32, (length, length), 1)
    return (1 - 2 * fold_parity(rows & cols, 8)).astype(F32).astype(BF16)


def split(value):
    high = value.astype(BF16)
    return high, (value - high.astype(F32)).astype(BF16)


def kernel(
    x_ref, cot_ref, bits_ref, row_ref, col_ref, out_ref,
    gbuf, xbuf, xt, bits, own_sign, far_sign, acc, table, rows, dot_sign, index_vmem, index, scale,
    terms, first, partial, second,
    a_send, a_recv, y_send, y_recv, x_send, x_recv, s_send, s_recv,
    b_send, b_recv, r_send, r_recv, c_send, c_recv, local_sem, w_send, w_recv, n_send, n_recv,
):
    wide, narrow, y_hi, z, core, y_lo, x = place()
    real = narrow != LAST

    def dev(y_hi=y_hi, z=z, core=core, y_lo=y_lo, x=x):
        return device(y_hi, z, core, y_lo, x)

    z_up, z_down, z_far = (z + 1) % 4, (z + 3) % 4, (z + 2) % 4
    barrier = pltpu.get_barrier_semaphore()
    peers = [(wide, narrow ^ offset) for offset in range(1, 8)]
    peers += [(wide ^ offset, narrow) for offset in range(1, 16)]
    peers += [dev(y_hi=1 - y_hi, y_lo=1 - y_lo)]
    for peer in peers:
        pl.semaphore_signal(barrier, inc=1, device_id=peer, device_id_type=MESH)

    def slot(z_at, core_at, offset):
        return pl.ds(pl.multiple_of(((z_at * 2 + core_at) * 8 + (narrow ^ offset)) * TOK, TOK), TOK)

    def columns(at):
        return pl.ds(pl.multiple_of(at * COLS, COLS), COLS)

    own_slice = cot_ref.at[0, 0, :, columns(narrow)]
    bits_copy = pltpu.make_async_copy(bits_ref.at[0], bits, local_sem.at[0])
    own_copy = pltpu.make_async_copy(own_slice, gbuf.at[slot(z, core, 0)], local_sem.at[1])
    index_copy = pltpu.make_async_copy(index_vmem, index, local_sem.at[2])
    bits_copy.start()

    @pl.when(real)
    def _():
        own_copy.start()

    row, col = row_ref[...], col_ref[...]
    index_vmem[...] = (col // 128) % 16 * 512 + row // 2048 * 256 + row % 256
    odd = fold_parity((wide & (row // 256)) ^ (narrow & (col // 2048)), 8)
    scale[...] = jnp.where(odd == 1, F32(-1.0), F32(1.0)) / jnp.sqrt(F32(8192))

    def ring_copy(direction, offset):
        landing = gbuf.at[slot(z, core, offset)]
        return remote(
            own_slice if offset == 0 else landing, landing,
            b_send.at[direction, offset], b_recv.at[direction, offset],
            dev(z=z_up if direction == 0 else z_down),
        )

    def relay_copy(direction, offset):
        source = z_down if direction == 0 else z_up
        base = ((source * 2 + core) * 8 + (narrow ^ offset)) * TOK + direction * (TOK // 2)
        span = gbuf.at[pl.ds(pl.multiple_of(base, TOK // 2), TOK // 2)]
        return remote(
            span, span, r_send.at[direction, offset], r_recv.at[direction, offset],
            dev(z=z_up if direction == 0 else z_down),
        )

    z_of = (z, z_down, z_far, z_up)

    def core_copy(distance, offset):
        landing = gbuf.at[slot(z_of[distance], core, offset)]
        return remote(
            own_slice if distance == 0 and offset == 0 else landing, landing,
            c_send.at[distance, offset], c_recv.at[distance, offset], dev(core=1 - core),
        )

    def pass_on(offset):
        ring_copy(0, offset).start()
        ring_copy(1, offset).start()
        core_copy(0, offset).start()

    pl.semaphore_wait(barrier, len(peers))

    @pl.when(real)
    def _():
        pass_on(0)

    def y_copy(target_lo):
        rel = y_hi ^ y_lo
        return remote(
            x_ref.at[0], xbuf.at[x, rel], y_send.at[target_lo], y_recv.at[rel],
            dev(y_hi=y_lo, y_lo=target_lo),
        )

    self_copy = pltpu.make_async_copy(x_ref.at[0], xbuf.at[x, 0], y_recv.at[0])
    for target_lo in range(2):
        mine = (y_hi == y_lo) & (y_lo == target_lo)

        @pl.when(mine)
        def _():
            self_copy.start()

        @pl.when(jnp.logical_not(mine))
        def _():
            y_copy(target_lo).start()

    def a_copy(offset):
        target = narrow ^ offset
        return remote(
            cot_ref.at[0, 0, :, columns(target)],
            gbuf.at[pl.ds(pl.multiple_of(((z * 2 + core) * 8 + narrow) * TOK, TOK), TOK)],
            a_send.at[offset], a_recv.at[offset],
            dev(y_lo=target // 4, x=target % 4),
        )

    order = (1, 3, 2, 4, 5, 7, 6)
    for offset in order:

        @pl.when((narrow ^ offset) != LAST)
        def _():
            a_copy(offset).start()

    index_copy.start()

    bits_copy.wait()

    @pl.loop(0, ROWS // 16)
    def _(step):
        span = pl.ds(pl.multiple_of(step * 16, 16), 16)
        own_sign[span, :] = (2 * bits[span, :] - 1).astype(F32).astype(BF16)

    sign_copy = remote(own_sign, far_sign, s_send.at[0], s_recv.at[0], dev(y_hi=1 - y_hi))

    def x_copy(rel, offset):
        return remote(
            xbuf.at[x, rel], xbuf.at[x, rel], x_send.at[rel, offset], x_recv.at[rel, offset],
            dev(x=x ^ offset),
        )

    def spread_inputs(rel):
        if rel == 0:
            @pl.when(y_hi == y_lo)
            def _():
                self_copy.wait()

            @pl.when(y_hi != y_lo)
            def _():
                remote(x_ref.at[0], xbuf.at[x, 0], y_send.at[0], y_recv.at[0], dev(y_lo=1 - y_lo)).wait_recv()
        else:
            remote(x_ref.at[0], xbuf.at[x, 1], y_send.at[0], y_recv.at[1], dev(y_lo=1 - y_lo)).wait_recv()
        for offset in (1, 3, 2):
            x_copy(rel, offset).start()

    lanes = lax.broadcasted_iota(I32, (128, 128), 1)

    def dot_signs(piece):
        for line in range(4 * piece, 4 * piece + 4):
            low = jnp.broadcast_to(col_ref[line:line + 1, :] % 128, (128, 128)).T
            dot_sign[line * 128:line * 128 + 128, :] = (1 - 2 * fold_parity(low & lanes, 4)).astype(F32).astype(BF16)

    def multiply(distance, start, last):
        z_at = z_of[distance]

        @pl.when(x != z_at)
        def _():
            for rel in range(2):
                landing = xbuf.at[z_at, rel]
                remote(landing, landing, x_send.at[rel, 1], x_recv.at[rel, x ^ z_at], dev(x=z_at)).wait_recv()

        for offset in range(8):
            core_copy(distance, offset).wait_recv()
        for rel in range(2):
            xt[rel * ROWS:(rel + 1) * ROWS, :] = xbuf[z_at, rel].T
        tokens = pl.ds(pl.multiple_of(z_at * 512, 512), 512)

        @pl.loop(0, COLS // 256)
        def _(tile):
            cols = pl.ds(pl.multiple_of(tile * 256, 256), 256)
            part = jnp.dot(xt[...], gbuf[tokens, cols], preferred_element_type=F32)
            for rel in range(2):
                value = part[rel * ROWS:(rel + 1) * ROWS]
                if not start:
                    value = value + acc[rel, :, cols]
                acc[rel, :, cols] = value

    def mix_rows(mix, rel, sign, cols):
        high, low = split(acc[rel, :, cols] * sign[:, cols].astype(F32))
        return jnp.dot(mix, high, preferred_element_type=F32) + jnp.dot(mix, low, preferred_element_type=F32)

    @pl.when(real)
    def _():
        sign_copy.start()
        for at, offset in enumerate(order):
            remote(
                own_slice, gbuf.at[slot(z, core, offset)], a_send.at[offset], a_recv.at[offset], dev(core=1 - core)
            ).wait_recv()
            pass_on(offset)
            if at in (2, 3):
                spread_inputs(at - 2)
            dot_signs(at)
        for at, offset in enumerate((0,) + order):
            for direction in range(2):
                landing = gbuf.at[slot(z_down if direction == 0 else z_up, core, offset)]
                remote(
                    landing, landing, b_send.at[direction, offset], b_recv.at[direction, offset], dev(z=z_up)
                ).wait_recv()
                relay_copy(direction, offset).start()
                core_copy(1 if direction == 0 else 3, offset).start()
            dot_signs(7 + at)
        own_copy.wait()
        multiply(0, True, False)
        multiply(1, False, False)
        multiply(3, False, False)
        dot_signs(15)
        for offset in (0,) + order:
            for direction in range(2):
                base = ((z_far * 2 + core) * 8 + (narrow ^ offset)) * TOK + direction * (TOK // 2)
                span = gbuf.at[pl.ds(pl.multiple_of(base, TOK // 2), TOK // 2)]
                remote(
                    span, span, r_send.at[direction, offset], r_recv.at[direction, offset], dev(z=z_up)
                ).wait_recv()
            core_copy(2, offset).start()
        multiply(2, False, True)

        mix = hadamard(ROWS)

        @pl.loop(0, 8)
        def _(tile):
            cols = pl.ds(pl.multiple_of(tile * 256, 256), 256)
            acc[0, :, cols] = mix_rows(mix, 0, own_sign, cols)

        sign_copy.wait_recv()

        @pl.loop(0, 8)
        def _(tile):
            cols = pl.ds(pl.multiple_of(tile * 256, 256), 256)
            near, far = acc[0, :, cols], mix_rows(mix, 1, far_sign, cols)
            for rel, value in ((0, near + far), (1, near - far)):
                left, right = value[:, :128], value[:, 128:]
                base = pl.multiple_of(tile * 1024 + rel * ROWS, ROWS)
                table[pl.ds(base, ROWS), :] = left + right
                table[pl.ds(base + 512, ROWS), :] = left - right

        @pl.loop(0, 64)
        def _(step):
            start = pl.multiple_of(step * 8, 8)
            for half in range(2):
                value = [table[pl.ds((2 * tile + half) * 512 + start, 8), :] for tile in range(8)]
                for bit in (1, 2, 4):
                    value = [
                        value[tile ^ bit] - value[tile] if tile & bit else value[tile] + value[tile | bit]
                        for tile in range(8)
                    ]
                for tile in range(8):
                    table[pl.ds((2 * tile + half) * 512 + start, 8), :] = value[tile]

        index_copy.wait()

        @pl.loop(0, 64)
        def _(line):
            base = pl.multiple_of(line * 128, 128)
            for i in range(128):
                rows[pl.ds(base + i, 1), :] = table[pl.ds(index[line, i], 1), :]

        ones = jnp.ones((8, 128), BF16)
        last_dims = (((1,), (1,)), ((), ()))

        @pl.loop(0, 16)
        def _(step):
            span = pl.ds(pl.multiple_of(step * 512, 512), 512)
            high, low = split(rows[span, :] * dot_sign[span, :].astype(F32))
            total = lax.dot_general(ones, high, last_dims, preferred_element_type=F32)
            total = total + lax.dot_general(ones, low, last_dims, preferred_element_type=F32)
            for part in range(4):
                terms[step, part:part + 1, :] = (
                    total[0:1, part * 128:(part + 1) * 128] * scale[pl.ds(step * 4 + part, 1), :]
                )

    @pl.when(jnp.logical_not(real))
    def _():
        index_copy.wait()
        terms[...] = jnp.zeros_like(terms)
        for rel in range(2):
            spread_inputs(rel)
        for offset in range(1, 4):
            for rel in range(2):
                landing = xbuf.at[x ^ offset, rel]
                remote(landing, landing, x_send.at[rel, 1], x_recv.at[rel, offset], dev(x=x ^ offset)).wait_recv()

    def wide_copy(offset):
        return remote(
            terms.at[wide ^ offset], first.at[offset], w_send.at[offset], w_recv.at[offset], (wide ^ offset, narrow)
        )

    def narrow_copy(offset):
        target = narrow ^ offset
        return remote(
            partial.at[target // 2], second.at[offset], n_send.at[offset], n_recv.at[offset], (wide, target)
        )

    for offset in range(1, 16):
        wide_copy(offset).start()
    total = terms[wide]
    for offset in range(1, 16):
        wide_copy(offset).wait_recv()
        total = total + first[offset]
    for line in range(4):
        partial[line] = total[line:line + 1]
    for offset in range(1, 8):
        narrow_copy(offset).start()
    line = partial[narrow // 2]
    for offset in range(1, 8):
        narrow_copy(offset).wait_recv()
        line = line + second[offset]
    out_ref[0] = jnp.where(narrow % 2 == 1, line[:, 64:], line[:, :64])

    @pl.when(real)
    def _():
        sign_copy.wait_send()
        for offset in range(8):
            for direction in range(2):
                ring_copy(direction, offset).wait_send()
                relay_copy(direction, offset).wait_send()
            for distance in range(4):
                core_copy(distance, offset).wait_send()

    for rel in range(2):
        for offset in (1, 3, 2):
            x_copy(rel, offset).wait_send()
    for target_lo in range(2):
        mine = (y_hi == y_lo) & (y_lo == target_lo)

        @pl.when(jnp.logical_not(mine))
        def _():
            y_copy(target_lo).wait_send()

    for offset in range(1, 8):

        @pl.when((narrow ^ offset) != LAST)
        def _():
            a_copy(offset).wait_send()

    for offset in range(1, 16):
        wide_copy(offset).wait_send()
    for offset in range(1, 8):
        narrow_copy(offset).wait_send()


def body(inputs, out_cotangent, sign_bits, row_pick, col_pick):
    hbm = pl.BlockSpec(memory_space=pl.ANY)
    vmem = pl.BlockSpec(memory_space=pltpu.VMEM)
    dma = pltpu.SemaphoreType.DMA
    return pl.pallas_call(
        kernel,
        out_shape=jax.ShapeDtypeStruct((1, 1, 64), F32),
        in_specs=[hbm, hbm, hbm, vmem, vmem],
        out_specs=vmem,
        scratch_shapes=[
            pltpu.VMEM((2048, COLS), BF16),
            pltpu.VMEM((4, 2, 512, ROWS), BF16),
            pltpu.VMEM((2 * ROWS, 512), BF16),
            pltpu.VMEM((ROWS, COLS), I32),
            pltpu.VMEM((ROWS, COLS), BF16),
            pltpu.VMEM((ROWS, COLS), BF16),
            pltpu.VMEM((2, ROWS, COLS), F32),
            pltpu.VMEM((8192, 128), F32),
            pltpu.VMEM((8192, 128), F32),
            pltpu.VMEM((8192, 128), BF16),
            pltpu.VMEM((64, 128), I32),
            pltpu.SMEM((64, 128), I32),
            pltpu.VMEM((64, 128), F32),
            pltpu.VMEM((16, 4, 128), F32),
            pltpu.VMEM((16, 4, 128), F32),
            pltpu.VMEM((4, 1, 128), F32),
            pltpu.VMEM((8, 1, 128), F32),
            dma((8,)), dma((8,)), dma((2,)), dma((2,)), dma((2, 4)), dma((2, 4)), dma((1,)), dma((1,)),
            dma((2, 8)), dma((2, 8)), dma((2, 8)), dma((2, 8)), dma((4, 8)), dma((4, 8)), dma((3,)),
            dma((16,)), dma((16,)), dma((8,)), dma((8,)),
        ],
        compiler_params=pltpu.CompilerParams(
            collective_id=0, has_side_effects=True, vmem_limit_bytes=VMEM_LIMIT
        ),
    )(inputs, out_cotangent, sign_bits, row_pick.reshape(64, 128), col_pick.reshape(64, 128))


def solution(mesh):
    return jax.shard_map(
        body,
        mesh=mesh,
        in_specs=(
            P(None, "narrow", "wide"),
            P(None, None, ("wide", "narrow"), None),
            P(None, "wide", "narrow"),
            P(),
            P(),
        ),
        out_specs=P(None, None, ("wide", "narrow")),
        check_vma=False,
    )
```

```python
import functools

import jax
import jax.numpy as jnp
from jax import lax
from jax.experimental import pallas as pl
from jax.experimental.pallas import tpu as pltpu
from jax.sharding import PartitionSpec as P

MESH = pl.DeviceIdType.MESH
F32 = jnp.float32
BF16 = jnp.bfloat16
I32 = jnp.int32
VMEM_LIMIT = 60 << 20

TOK = 32
COLS = 2048
ROWS = 256
SLICES = ((0, 1), (3, 2), (4, 5), (7,), (6,))
MULTIPLY_AT = (7, 9, 11, 12, 12)
LAST = 7


def place():
    wide = lax.axis_index("wide")
    narrow = lax.axis_index("narrow")
    return wide, narrow, wide // 8, (wide // 2) % 4, wide % 2, narrow // 4, narrow % 4


def device(y_hi, z, core, y_lo, x):
    return (y_hi * 8 + z * 2 + core, y_lo * 4 + x)


def remote(src, dst, send, recv, target):
    return pltpu.make_async_remote_copy(
        src_ref=src, dst_ref=dst, send_sem=send, recv_sem=recv, device_id=target, device_id_type=MESH
    )


def fold_parity(value, top):
    while top:
        value = value ^ (value >> top)
        top //= 2
    return value & 1


def hadamard(length):
    rows = lax.broadcasted_iota(I32, (length, length), 0)
    cols = lax.broadcasted_iota(I32, (length, length), 1)
    return (1 - 2 * fold_parity(rows & cols, 8)).astype(F32).astype(BF16)


def split(value):
    high = value.astype(BF16)
    return high, (value - high.astype(F32)).astype(BF16)


def kernel(
    inputs, cot_ref, bits_ref, row_ref, col_ref, out_ref,
    gbuf, xbuf, xt, bits, own_sign, far_sign, acc, table, rows, dot_sign, index_vmem, index, scale,
    terms, first, partial, second,
    a_send, a_recv, y_send, y_recv, x_send, x_recv, h_send, h_recv, s_send, s_recv,
    b_send, b_recv, r_send, r_recv, c_send, c_recv, local_sem, w_send, w_recv, n_send, n_recv,
):
    wide, narrow, y_hi, z, core, y_lo, x = place()
    real = narrow != LAST

    def dev(y_hi=y_hi, z=z, core=core, y_lo=y_lo, x=x):
        return device(y_hi, z, core, y_lo, x)

    z_up, z_down, z_far = (z + 1) % 4, (z + 3) % 4, (z + 2) % 4
    barrier = pltpu.get_barrier_semaphore()
    peers = [(wide, narrow ^ offset) for offset in range(1, 8)]
    peers += [(wide ^ offset, narrow) for offset in range(1, 16)]
    peers += [dev(y_hi=1 - y_hi, y_lo=1 - y_lo)]
    for peer in peers:
        pl.semaphore_signal(barrier, inc=1, device_id=peer, device_id_type=MESH)

    def slot(z_at, core_at, offset):
        return gbuf.at[z_at * 2 + core_at, pl.ds(pl.multiple_of((narrow ^ offset) * TOK, TOK), TOK)]

    def half_slot(direction, z_at, offset):
        base = (narrow ^ offset) * TOK + direction * (TOK // 2)
        return gbuf.at[z_at * 2 + core, pl.ds(pl.multiple_of(base, TOK // 2), TOK // 2)]

    def columns(at):
        return pl.ds(pl.multiple_of(at * COLS, COLS), COLS)

    own_slice = cot_ref.at[0, 0, :, columns(narrow)]
    bits_copy = pltpu.make_async_copy(bits_ref.at[0], bits, local_sem.at[0])
    own_copy = pltpu.make_async_copy(own_slice, slot(z, core, 0), local_sem.at[1])
    index_copy = pltpu.make_async_copy(index_vmem, index, local_sem.at[2])
    bits_copy.start()

    @pl.when(real)
    def _():
        own_copy.start()

    row, col = row_ref[...], col_ref[...]
    index_vmem[...] = (col // 128) % 16 * 512 + row // 2048 * 256 + row % 256
    odd = fold_parity((wide & (row // 256)) ^ (narrow & (col // 2048)), 8)
    scale[...] = jnp.where(odd == 1, F32(-1.0), F32(1.0)) / jnp.sqrt(F32(8192))

    def ring_copy(direction, offset):
        landing = slot(z, core, offset)
        return remote(
            own_slice if offset == 0 else landing, landing,
            b_send.at[direction, offset], b_recv.at[direction, offset],
            dev(z=z_up if direction == 0 else z_down),
        )

    def relay_copy(direction, offset):
        span = half_slot(direction, z_down if direction == 0 else z_up, offset)
        return remote(
            span, span, r_send.at[direction, offset], r_recv.at[direction, offset],
            dev(z=z_up if direction == 0 else z_down),
        )

    z_of = (z, z_down, z_far, z_up)

    def core_copy(distance, offset):
        landing = slot(z_of[distance], core, offset)
        return remote(
            own_slice if distance == 0 and offset == 0 else landing, landing,
            c_send.at[distance, offset], c_recv.at[distance, offset], dev(core=1 - core),
        )

    def pass_on(offset):
        ring_copy(0, offset).start()
        ring_copy(1, offset).start()
        core_copy(0, offset).start()

    pl.semaphore_wait(barrier, len(peers))

    @pl.when(real)
    def _():
        pass_on(0)

    def y_copy(target_lo):
        rel = y_hi ^ y_lo
        return remote(
            inputs, xbuf.at[x, rel], y_send.at[target_lo], y_recv.at[rel],
            dev(y_hi=y_lo, y_lo=target_lo),
        )

    self_copy = pltpu.make_async_copy(inputs, xbuf.at[x, 0], y_recv.at[0])
    for target_lo in range(2):
        mine = (y_hi == y_lo) & (y_lo == target_lo)

        @pl.when(mine)
        def _():
            self_copy.start()

        @pl.when(jnp.logical_not(mine))
        def _():
            y_copy(target_lo).start()

    def a_copy(offset):
        target = narrow ^ offset
        return remote(
            cot_ref.at[0, 0, :, columns(target)],
            slot(z, core, 0),
            a_send.at[offset], a_recv.at[offset],
            dev(y_lo=target // 4, x=target % 4),
        )

    order = (0, 1, 3, 2, 4, 5, 7, 6)

    def send_cotangents(offsets):
        for offset in offsets:

            @pl.when((narrow ^ offset) != LAST)
            def _():
                a_copy(offset).start()

    send_cotangents(order[1:5])

    index_copy.start()

    bits_copy.wait()

    @pl.loop(0, ROWS // 16)
    def _(step):
        span = pl.ds(pl.multiple_of(step * 16, 16), 16)
        own_sign[span, :] = (2 * bits[span, :] - 1).astype(F32).astype(BF16)

    sign_copy = remote(own_sign, far_sign, s_send.at[0], s_recv.at[0], dev(y_hi=1 - y_hi))

    def x_copy(rel, offset):
        block = xbuf.at[x, rel]
        return remote(block, block, x_send.at[rel, offset], x_recv.at[rel, offset], dev(x=x ^ offset))

    def x_relay(rel, half):
        block = xbuf.at[x ^ (1 + 2 * half), rel, half]
        return remote(block, block, h_send.at[rel, half], h_recv.at[rel, half], dev(x=x ^ (3 - 2 * half)))

    def spread_inputs(rel):
        if rel == 0:
            @pl.when(y_hi == y_lo)
            def _():
                self_copy.wait()

            @pl.when(y_hi != y_lo)
            def _():
                remote(inputs, xbuf.at[x, 0], y_send.at[0], y_recv.at[0], dev(y_lo=1 - y_lo)).wait_recv()
        else:
            remote(inputs, xbuf.at[x, 1], y_send.at[0], y_recv.at[1], dev(y_lo=1 - y_lo)).wait_recv()
        for offset in (1, 3):
            x_copy(rel, offset).start()

    def relay_inputs(rel):
        for half in range(2):
            block = xbuf.at[x ^ (1 + 2 * half), rel]
            remote(
                block, block, x_send.at[rel, 1], x_recv.at[rel, 1 + 2 * half], dev(x=x ^ 1)
            ).wait_recv()
            x_relay(rel, half).start()

    def await_inputs():
        for rel in range(2):
            for half in range(2):
                block = xbuf.at[x ^ 2, rel, half]
                remote(block, block, h_send.at[rel, half], h_recv.at[rel, half], dev(x=x ^ 1)).wait_recv()

    lanes = lax.broadcasted_iota(I32, (128, 128), 1)

    def dot_signs(piece):
        for line in range(4 * piece, 4 * piece + 4):
            low = jnp.broadcast_to(col_ref[line:line + 1, :] % 128, (128, 128)).T
            dot_sign[line * 128:line * 128 + 128, :] = (1 - 2 * fold_parity(low & lanes, 4)).astype(F32).astype(BF16)

    def multiply(offsets):
        for distance in range(4):
            for offset in offsets:
                core_copy(distance, offset).wait_recv()
        size = len(offsets) * TOK
        tokens = pl.ds(pl.multiple_of((narrow ^ offsets[0]) // len(offsets) * size, size), size)
        depth = 8 * size
        for rel in range(2):
            xt[rel * ROWS:(rel + 1) * ROWS, :depth] = xbuf[:, rel, :, tokens, :].reshape(depth, ROWS).T

        @pl.loop(0, COLS // 256)
        def _(tile):
            cols = pl.ds(pl.multiple_of(tile * 256, 256), 256)
            part = jnp.dot(xt[:, :depth], gbuf[:, tokens, cols].reshape(depth, 256), preferred_element_type=F32)
            for rel in range(2):
                value = part[rel * ROWS:(rel + 1) * ROWS]
                if 0 not in offsets:
                    value = value + acc[rel, :, cols]
                acc[rel, :, cols] = value

    def wide_copy(offset):
        return remote(
            terms.at[wide ^ offset], first.at[offset], w_send.at[offset], w_recv.at[offset], (wide ^ offset, narrow)
        )

    def mix_rows(mix, rel, sign, cols):
        high, low = split(acc[rel, :, cols] * sign[:, cols].astype(F32))
        return jnp.dot(mix, high, preferred_element_type=F32) + jnp.dot(mix, low, preferred_element_type=F32)

    @pl.when(real)
    def _():
        sign_copy.start()
        for step in range(1, 13):
            if step < 8:
                remote(
                    own_slice, slot(z, core, order[step]), a_send.at[order[step]], a_recv.at[order[step]],
                    dev(core=1 - core),
                ).wait_recv()
                pass_on(order[step])
            if step in (2, 3):
                spread_inputs(step - 2)
                send_cotangents(order[5:6] if step == 2 else order[6:])
            if step in (4, 5):
                relay_inputs(step - 4)
            if 0 <= step - 2 < 8:
                offset = order[step - 2]
                for direction in range(2):
                    landing = slot(z_down if direction == 0 else z_up, core, offset)
                    remote(
                        landing, landing, b_send.at[direction, offset], b_recv.at[direction, offset], dev(z=z_up)
                    ).wait_recv()
                    relay_copy(direction, offset).start()
                    core_copy(1 if direction == 0 else 3, offset).start()
            if 0 <= step - 5 < 8:
                offset = order[step - 5]
                for direction in range(2):
                    span = half_slot(direction, z_far, offset)
                    remote(
                        span, span, r_send.at[direction, offset], r_recv.at[direction, offset], dev(z=z_up)
                    ).wait_recv()
                core_copy(2, offset).start()
            if step <= 8:
                dot_signs(2 * step - 2)
                dot_signs(2 * step - 1)
            if step == MULTIPLY_AT[0]:
                own_copy.wait()
                await_inputs()
            for at, offsets in zip(MULTIPLY_AT, SLICES, strict=True):
                if step == at:
                    multiply(offsets)

        mix = hadamard(ROWS)

        @pl.loop(0, 8)
        def _(tile):
            cols = pl.ds(pl.multiple_of(tile * 256, 256), 256)
            acc[0, :, cols] = mix_rows(mix, 0, own_sign, cols)

        sign_copy.wait_recv()

        @pl.loop(0, 8)
        def _(tile):
            cols = pl.ds(pl.multiple_of(tile * 256, 256), 256)
            near, far = acc[0, :, cols], mix_rows(mix, 1, far_sign, cols)
            for rel, value in ((0, near + far), (1, near - far)):
                left, right = value[:, :128], value[:, 128:]
                base = pl.multiple_of(tile * 1024 + rel * ROWS, ROWS)
                table[pl.ds(base, ROWS), :] = left + right
                table[pl.ds(base + 512, ROWS), :] = left - right

        @pl.loop(0, 64)
        def _(step):
            start = pl.multiple_of(step * 8, 8)
            for half in range(2):
                value = [table[pl.ds((2 * tile + half) * 512 + start, 8), :] for tile in range(8)]
                for bit in (1, 2, 4):
                    value = [
                        value[tile ^ bit] - value[tile] if tile & bit else value[tile] + value[tile | bit]
                        for tile in range(8)
                    ]
                for tile in range(8):
                    table[pl.ds((2 * tile + half) * 512 + start, 8), :] = value[tile]

        index_copy.wait()
        ones = jnp.ones((8, 256), BF16)
        last_dims = (((1,), (1,)), ((), ()))

        def dot_rows(block, held):
            span = pl.ds(pl.multiple_of(block * 512, 512), 512)
            both = jnp.concatenate(split(held[...] * dot_sign[span, :].astype(F32)), axis=1)
            total = lax.dot_general(ones, both, last_dims, preferred_element_type=F32)
            for part in range(4):
                terms[block, part:part + 1, :] = (
                    total[0:1, part * 128:(part + 1) * 128] * scale[pl.ds(block * 4 + part, 1), :]
                )

        @pl.loop(0, 16)
        def _(step):
            block = wide ^ (15 - step)

            @pl.loop(0, 4)
            def _(part):
                base = pl.multiple_of(part * 128, 128)
                for i in range(128):
                    rows[0, pl.ds(base + i, 1), :] = table[pl.ds(index[block * 4 + part, i], 1), :]

            dot_rows(block, rows.at[0])

            @pl.when(step < 15)
            def _():
                wide_copy(15 - step).start()

    @pl.when(jnp.logical_not(real))
    def _():
        index_copy.wait()
        terms[...] = jnp.zeros_like(terms)

        @pl.loop(1, 16)
        def _(step):
            wide_copy(16 - step).start()

        for rel in range(2):
            spread_inputs(rel)
            send_cotangents(order[5:6] if rel == 0 else order[6:])
        for rel in range(2):
            relay_inputs(rel)
        await_inputs()

    def narrow_copy(offset):
        target = narrow ^ offset
        return remote(
            partial.at[target // 2], second.at[offset], n_send.at[offset], n_recv.at[offset], (wide, target)
        )

    total = terms[wide]
    for offset in range(15, 0, -1):
        wide_copy(offset).wait_recv()
        total = total + first[offset]
    for line in range(4):
        partial[line] = total[line:line + 1]
    for offset in range(1, 8):
        narrow_copy(offset).start()
    line = partial[narrow // 2]
    for offset in range(1, 8):
        narrow_copy(offset).wait_recv()
        line = line + second[offset]
    out_ref[0] = jnp.where(narrow % 2 == 1, line[:, 64:], line[:, :64])

    @pl.when(real)
    def _():
        sign_copy.wait_send()
        for offset in order:
            for direction in range(2):
                ring_copy(direction, offset).wait_send()
                relay_copy(direction, offset).wait_send()
            for distance in range(4):
                core_copy(distance, offset).wait_send()

    for rel in range(2):
        for half in range(2):
            x_copy(rel, 1 + 2 * half).wait_send()
            x_relay(rel, half).wait_send()
    for target_lo in range(2):
        mine = (y_hi == y_lo) & (y_lo == target_lo)

        @pl.when(jnp.logical_not(mine))
        def _():
            y_copy(target_lo).wait_send()

    for offset in range(1, 8):

        @pl.when((narrow ^ offset) != LAST)
        def _():
            a_copy(offset).wait_send()

    for offset in range(1, 16):
        wide_copy(offset).wait_send()
    for offset in range(1, 8):
        narrow_copy(offset).wait_send()


def body(inputs, out_cotangent, sign_bits, row_pick, col_pick):
    hbm = pl.BlockSpec(memory_space=pl.ANY)
    vmem = pl.BlockSpec(memory_space=pltpu.VMEM)
    dma = pltpu.SemaphoreType.DMA
    return pl.pallas_call(
        kernel,
        out_shape=jax.ShapeDtypeStruct((1, 1, 64), F32),
        in_specs=[hbm, hbm, hbm, vmem, vmem],
        out_specs=vmem,
        scratch_shapes=[
            pltpu.VMEM((8, 8 * TOK, COLS), BF16),
            pltpu.VMEM((4, 2, 2, 8 * TOK, ROWS), BF16),
            pltpu.VMEM((2 * ROWS, 512), BF16),
            pltpu.VMEM((ROWS, COLS), I32),
            pltpu.VMEM((ROWS, COLS), BF16),
            pltpu.VMEM((ROWS, COLS), BF16),
            pltpu.VMEM((2, ROWS, COLS), F32),
            pltpu.VMEM((8192, 128), F32),
            pltpu.VMEM((2, 512, 128), F32),
            pltpu.VMEM((8192, 128), BF16),
            pltpu.VMEM((64, 128), I32),
            pltpu.SMEM((64, 128), I32),
            pltpu.VMEM((64, 128), F32),
            pltpu.VMEM((16, 4, 128), F32),
            pltpu.VMEM((16, 4, 128), F32),
            pltpu.VMEM((4, 1, 128), F32),
            pltpu.VMEM((8, 1, 128), F32),
            dma((8,)), dma((8,)), dma((2,)), dma((2,)), dma((2, 4)), dma((2, 4)), dma((2, 2)), dma((2, 2)), dma((1,)), dma((1,)),
            dma((2, 8)), dma((2, 8)), dma((2, 8)), dma((2, 8)), dma((4, 8)), dma((4, 8)), dma((3,)),
            dma((16,)), dma((16,)), dma((8,)), dma((8,)),
        ],
        compiler_params=pltpu.CompilerParams(
            collective_id=0, has_side_effects=True, vmem_limit_bytes=VMEM_LIMIT
        ),
    )(inputs.reshape(2, 8 * TOK, ROWS), out_cotangent, sign_bits, row_pick.reshape(64, 128), col_pick.reshape(64, 128))


def solution(mesh):
    return jax.shard_map(
        body,
        mesh=mesh,
        in_specs=(
            P(None, "narrow", "wide"),
            P(None, None, ("wide", "narrow"), None),
            P(None, "wide", "narrow"),
            P(),
            P(),
        ),
        out_specs=P(None, None, ("wide", "narrow")),
        check_vma=False,
    )
```

```python
import functools

import jax
import jax.numpy as jnp
from jax import lax
from jax.experimental import pallas as pl
from jax.experimental.pallas import tpu as pltpu
from jax.sharding import PartitionSpec as P

MESH = pl.DeviceIdType.MESH
F32 = jnp.float32
BF16 = jnp.bfloat16
I32 = jnp.int32
VMEM_LIMIT = 60 << 20

TOK = 32
COLS = 2048
ROWS = 256
SLICES = ((0, 1), (3, 2), (4, 5), (7,), (6,))
MULTIPLY_AT = (7, 9, 11, 12, 12)
LAST = 7


def place():
    wide = lax.axis_index("wide")
    narrow = lax.axis_index("narrow")
    return wide, narrow, wide // 8, (wide // 2) % 4, wide % 2, narrow // 4, narrow % 4


def device(y_hi, z, core, y_lo, x):
    return (y_hi * 8 + z * 2 + core, y_lo * 4 + x)


def remote(src, dst, send, recv, target):
    return pltpu.make_async_remote_copy(
        src_ref=src, dst_ref=dst, send_sem=send, recv_sem=recv, device_id=target, device_id_type=MESH
    )


def fold_parity(value, top):
    while top:
        value = value ^ (value >> top)
        top //= 2
    return value & 1


def hadamard(length):
    rows = lax.broadcasted_iota(I32, (length, length), 0)
    cols = lax.broadcasted_iota(I32, (length, length), 1)
    return (1 - 2 * fold_parity(rows & cols, 8)).astype(F32).astype(BF16)


def split(value):
    high = value.astype(BF16)
    return high, (value - high.astype(F32)).astype(BF16)


def kernel(
    inputs, cot_ref, bits_ref, row_ref, col_ref, out_ref,
    gbuf, xbuf, xt, bits, own_sign, far_sign, acc, table, rows, dot_sign, index_vmem, index, scale,
    terms, first, partial, second,
    a_send, a_recv, y_send, y_recv, x_send, x_recv, h_send, h_recv, s_send, s_recv,
    b_send, b_recv, r_send, r_recv, c_send, c_recv, local_sem, w_send, w_recv, n_send, n_recv,
):
    wide, narrow, y_hi, z, core, y_lo, x = place()
    real = narrow != LAST

    def dev(y_hi=y_hi, z=z, core=core, y_lo=y_lo, x=x):
        return device(y_hi, z, core, y_lo, x)

    z_up, z_down, z_far = (z + 1) % 4, (z + 3) % 4, (z + 2) % 4
    barrier = pltpu.get_barrier_semaphore()
    peers = [(wide, narrow ^ offset) for offset in range(1, 8)]
    peers += [(wide ^ offset, narrow) for offset in range(1, 16)]
    peers += [dev(y_hi=1 - y_hi, y_lo=1 - y_lo)]
    for peer in peers:
        pl.semaphore_signal(barrier, inc=1, device_id=peer, device_id_type=MESH)

    def slot(z_at, core_at, offset):
        return gbuf.at[z_at * 2 + core_at, pl.ds(pl.multiple_of((narrow ^ offset) * TOK, TOK), TOK)]

    def half_slot(direction, z_at, offset):
        base = (narrow ^ offset) * TOK + direction * (TOK // 2)
        return gbuf.at[z_at * 2 + core, pl.ds(pl.multiple_of(base, TOK // 2), TOK // 2)]

    def columns(at):
        return pl.ds(pl.multiple_of(at * COLS, COLS), COLS)

    own_slice = cot_ref.at[0, 0, :, columns(narrow)]
    bits_copy = pltpu.make_async_copy(bits_ref.at[0], bits, local_sem.at[0])
    own_copy = pltpu.make_async_copy(own_slice, slot(z, core, 0), local_sem.at[1])
    index_copy = pltpu.make_async_copy(index_vmem, index, local_sem.at[2])
    bits_copy.start()

    @pl.when(real)
    def _():
        own_copy.start()

    row, col = row_ref[...], col_ref[...]
    index_vmem[...] = (col // 128) % 16 * 512 + row // 2048 * 256 + row % 256
    odd = fold_parity((wide & (row // 256)) ^ (narrow & (col // 2048)), 8)
    scale[...] = jnp.where(odd == 1, F32(-1.0), F32(1.0)) / jnp.sqrt(F32(8192))

    def ring_copy(direction, offset):
        landing = slot(z, core, offset)
        return remote(
            own_slice if offset == 0 else landing, landing,
            b_send.at[direction, offset], b_recv.at[direction, offset],
            dev(z=z_up if direction == 0 else z_down),
        )

    def relay_copy(direction, offset):
        span = half_slot(direction, z_down if direction == 0 else z_up, offset)
        return remote(
            span, span, r_send.at[direction, offset], r_recv.at[direction, offset],
            dev(z=z_up if direction == 0 else z_down),
        )

    z_of = (z, z_down, z_far, z_up)

    def core_copy(distance, offset):
        landing = slot(z_of[distance], core, offset)
        return remote(
            own_slice if distance == 0 and offset == 0 else landing, landing,
            c_send.at[distance, offset], c_recv.at[distance, offset], dev(core=1 - core),
        )

    def pass_on(offset):
        ring_copy(0, offset).start()
        ring_copy(1, offset).start()
        core_copy(0, offset).start()

    pl.semaphore_wait(barrier, len(peers))

    @pl.when(real)
    def _():
        pass_on(0)

    def y_copy(target_lo):
        rel = y_hi ^ y_lo
        return remote(
            inputs, xbuf.at[x, rel], y_send.at[target_lo], y_recv.at[rel],
            dev(y_hi=y_lo, y_lo=target_lo),
        )

    self_copy = pltpu.make_async_copy(inputs, xbuf.at[x, 0], y_recv.at[0])
    for target_lo in range(2):
        mine = (y_hi == y_lo) & (y_lo == target_lo)

        @pl.when(mine)
        def _():
            self_copy.start()

        @pl.when(jnp.logical_not(mine))
        def _():
            y_copy(target_lo).start()

    def a_copy(offset):
        target = narrow ^ offset
        return remote(
            cot_ref.at[0, 0, :, columns(target)],
            slot(z, core, 0),
            a_send.at[offset], a_recv.at[offset],
            dev(y_lo=target // 4, x=target % 4),
        )

    order = (0, 1, 3, 2, 4, 5, 7, 6)

    def send_cotangents(offsets):
        for offset in offsets:

            @pl.when((narrow ^ offset) != LAST)
            def _():
                a_copy(offset).start()

    send_cotangents(order[1:5])

    index_copy.start()

    bits_copy.wait()

    @pl.loop(0, ROWS // 16)
    def _(step):
        span = pl.ds(pl.multiple_of(step * 16, 16), 16)
        own_sign[span, :] = (2 * bits[span, :] - 1).astype(F32).astype(BF16)

    sign_copy = remote(own_sign, far_sign, s_send.at[0], s_recv.at[0], dev(y_hi=1 - y_hi))

    def x_copy(rel, offset):
        block = xbuf.at[x, rel]
        return remote(block, block, x_send.at[rel, offset], x_recv.at[rel, offset], dev(x=x ^ offset))

    def x_relay(rel, half):
        block = xbuf.at[x ^ (1 + 2 * half), rel, half]
        return remote(block, block, h_send.at[rel, half], h_recv.at[rel, half], dev(x=x ^ (3 - 2 * half)))

    def spread_inputs(rel):
        if rel == 0:
            @pl.when(y_hi == y_lo)
            def _():
                self_copy.wait()

            @pl.when(y_hi != y_lo)
            def _():
                remote(inputs, xbuf.at[x, 0], y_send.at[0], y_recv.at[0], dev(y_lo=1 - y_lo)).wait_recv()
        else:
            remote(inputs, xbuf.at[x, 1], y_send.at[0], y_recv.at[1], dev(y_lo=1 - y_lo)).wait_recv()
        for offset in (1, 3):
            x_copy(rel, offset).start()

    def relay_inputs(rel):
        for half in range(2):
            block = xbuf.at[x ^ (1 + 2 * half), rel]
            remote(
                block, block, x_send.at[rel, 1], x_recv.at[rel, 1 + 2 * half], dev(x=x ^ 1)
            ).wait_recv()
            x_relay(rel, half).start()

    def await_inputs():
        for rel in range(2):
            for half in range(2):
                block = xbuf.at[x ^ 2, rel, half]
                remote(block, block, h_send.at[rel, half], h_recv.at[rel, half], dev(x=x ^ 1)).wait_recv()

    lanes = lax.broadcasted_iota(I32, (128, 128), 1)

    def dot_signs(piece):
        for line in range(4 * piece, 4 * piece + 4):
            low = jnp.broadcast_to(col_ref[line:line + 1, :] % 128, (128, 128)).T
            dot_sign[line * 128:line * 128 + 128, :] = (1 - 2 * fold_parity(low & lanes, 4)).astype(F32).astype(BF16)

    def multiply(offsets):
        for distance in range(4):
            for offset in offsets:
                core_copy(distance, offset).wait_recv()
        size = len(offsets) * TOK
        tokens = pl.ds(pl.multiple_of((narrow ^ offsets[0]) // len(offsets) * size, size), size)
        depth = 8 * size
        for rel in range(2):
            xt[rel * ROWS:(rel + 1) * ROWS, :depth] = xbuf[:, rel, :, tokens, :].reshape(depth, ROWS).T

        @pl.loop(0, COLS // 256)
        def _(tile):
            cols = pl.ds(pl.multiple_of(tile * 256, 256), 256)
            part = jnp.dot(xt[:, :depth], gbuf[:, tokens, cols].reshape(depth, 256), preferred_element_type=F32)
            for rel in range(2):
                value = part[rel * ROWS:(rel + 1) * ROWS]
                if 0 not in offsets:
                    value = value + acc[rel, :, cols]
                acc[rel, :, cols] = value

    def wide_copy(offset):
        return remote(
            terms.at[wide ^ offset], first.at[offset], w_send.at[offset], w_recv.at[offset], (wide ^ offset, narrow)
        )

    def mix_rows(mix, rel, sign, cols):
        both = jnp.concatenate(split(acc[rel, :, cols] * sign[:, cols].astype(F32)), axis=0)
        return jnp.dot(mix, both, preferred_element_type=F32)

    @pl.when(real)
    def _():
        sign_copy.start()
        for step in range(1, 13):
            if step < 8:
                remote(
                    own_slice, slot(z, core, order[step]), a_send.at[order[step]], a_recv.at[order[step]],
                    dev(core=1 - core),
                ).wait_recv()
                pass_on(order[step])
            if step in (2, 3):
                spread_inputs(step - 2)
                send_cotangents(order[5:6] if step == 2 else order[6:])
            if step in (4, 5):
                relay_inputs(step - 4)
            if 0 <= step - 2 < 8:
                offset = order[step - 2]
                for direction in range(2):
                    landing = slot(z_down if direction == 0 else z_up, core, offset)
                    remote(
                        landing, landing, b_send.at[direction, offset], b_recv.at[direction, offset], dev(z=z_up)
                    ).wait_recv()
                    relay_copy(direction, offset).start()
                    core_copy(1 if direction == 0 else 3, offset).start()
            if 0 <= step - 5 < 8:
                offset = order[step - 5]
                for direction in range(2):
                    span = half_slot(direction, z_far, offset)
                    remote(
                        span, span, r_send.at[direction, offset], r_recv.at[direction, offset], dev(z=z_up)
                    ).wait_recv()
                core_copy(2, offset).start()
            if step <= 8:
                dot_signs(2 * step - 2)
                dot_signs(2 * step - 1)
            if step == MULTIPLY_AT[0]:
                own_copy.wait()
                await_inputs()
            for at, offsets in zip(MULTIPLY_AT, SLICES, strict=True):
                if step == at:
                    multiply(offsets)

        mix = jnp.concatenate([hadamard(ROWS)] * 2, axis=1)

        @pl.loop(0, 8)
        def _(tile):
            cols = pl.ds(pl.multiple_of(tile * 256, 256), 256)
            acc[0, :, cols] = mix_rows(mix, 0, own_sign, cols)

        sign_copy.wait_recv()

        @pl.loop(0, 8)
        def _(tile):
            cols = pl.ds(pl.multiple_of(tile * 256, 256), 256)
            near, far = acc[0, :, cols], mix_rows(mix, 1, far_sign, cols)
            for rel, value in ((0, near + far), (1, near - far)):
                left, right = value[:, :128], value[:, 128:]
                base = pl.multiple_of(tile * 1024 + rel * ROWS, ROWS)
                table[pl.ds(base, ROWS), :] = left + right
                table[pl.ds(base + 512, ROWS), :] = left - right

        @pl.loop(0, 64)
        def _(step):
            start = pl.multiple_of(step * 8, 8)
            for half in range(2):
                value = [table[pl.ds((2 * tile + half) * 512 + start, 8), :] for tile in range(8)]
                for bit in (1, 2, 4):
                    value = [
                        value[tile ^ bit] - value[tile] if tile & bit else value[tile] + value[tile | bit]
                        for tile in range(8)
                    ]
                for tile in range(8):
                    table[pl.ds((2 * tile + half) * 512 + start, 8), :] = value[tile]

        index_copy.wait()

        def dot_rows(block, held):
            span = pl.ds(pl.multiple_of(block * 512, 512), 512)
            total = jnp.sum((held[...] * dot_sign[span, :].astype(F32)).T, axis=0, keepdims=True)
            for part in range(4):
                terms[block, part:part + 1, :] = (
                    total[:, part * 128:(part + 1) * 128] * scale[pl.ds(block * 4 + part, 1), :]
                )

        @pl.loop(0, 16)
        def _(step):
            block = wide ^ (15 - step)

            @pl.loop(0, 4)
            def _(part):
                base = pl.multiple_of(part * 128, 128)
                for i in range(128):
                    rows[0, pl.ds(base + i, 1), :] = table[pl.ds(index[block * 4 + part, i], 1), :]

            dot_rows(block, rows.at[0])

            @pl.when(step < 15)
            def _():
                wide_copy(15 - step).start()

    @pl.when(jnp.logical_not(real))
    def _():
        index_copy.wait()
        terms[...] = jnp.zeros_like(terms)

        @pl.loop(1, 16)
        def _(step):
            wide_copy(16 - step).start()

        for rel in range(2):
            spread_inputs(rel)
            send_cotangents(order[5:6] if rel == 0 else order[6:])
        for rel in range(2):
            relay_inputs(rel)
        await_inputs()

    def narrow_copy(offset):
        target = narrow ^ offset
        return remote(
            partial.at[target // 2], second.at[offset], n_send.at[offset], n_recv.at[offset], (wide, target)
        )

    total = terms[wide]
    for offset in range(15, 0, -1):
        wide_copy(offset).wait_recv()
        total = total + first[offset]
    for line in range(4):
        partial[line] = total[line:line + 1]
    for offset in range(1, 8):
        narrow_copy(offset).start()
    line = partial[narrow // 2]
    for offset in range(1, 8):
        narrow_copy(offset).wait_recv()
        line = line + second[offset]
    out_ref[0] = jnp.where(narrow % 2 == 1, line[:, 64:], line[:, :64])

    @pl.when(real)
    def _():
        sign_copy.wait_send()
        for offset in order:
            for direction in range(2):
                ring_copy(direction, offset).wait_send()
                relay_copy(direction, offset).wait_send()
            for distance in range(4):
                core_copy(distance, offset).wait_send()

    for rel in range(2):
        for half in range(2):
            x_copy(rel, 1 + 2 * half).wait_send()
            x_relay(rel, half).wait_send()
    for target_lo in range(2):
        mine = (y_hi == y_lo) & (y_lo == target_lo)

        @pl.when(jnp.logical_not(mine))
        def _():
            y_copy(target_lo).wait_send()

    for offset in range(1, 8):

        @pl.when((narrow ^ offset) != LAST)
        def _():
            a_copy(offset).wait_send()

    for offset in range(1, 16):
        wide_copy(offset).wait_send()
    for offset in range(1, 8):
        narrow_copy(offset).wait_send()


def body(inputs, out_cotangent, sign_bits, row_pick, col_pick):
    hbm = pl.BlockSpec(memory_space=pl.ANY)
    vmem = pl.BlockSpec(memory_space=pltpu.VMEM)
    dma = pltpu.SemaphoreType.DMA
    return pl.pallas_call(
        kernel,
        out_shape=jax.ShapeDtypeStruct((1, 1, 64), F32),
        in_specs=[hbm, hbm, hbm, vmem, vmem],
        out_specs=vmem,
        scratch_shapes=[
            pltpu.VMEM((8, 8 * TOK, COLS), BF16),
            pltpu.VMEM((4, 2, 2, 8 * TOK, ROWS), BF16),
            pltpu.VMEM((2 * ROWS, 512), BF16),
            pltpu.VMEM((ROWS, COLS), I32),
            pltpu.VMEM((ROWS, COLS), BF16),
            pltpu.VMEM((ROWS, COLS), BF16),
            pltpu.VMEM((2, ROWS, COLS), F32),
            pltpu.VMEM((8192, 128), F32),
            pltpu.VMEM((2, 512, 128), F32),
            pltpu.VMEM((8192, 128), BF16),
            pltpu.VMEM((64, 128), I32),
            pltpu.SMEM((64, 128), I32),
            pltpu.VMEM((64, 128), F32),
            pltpu.VMEM((16, 4, 128), F32),
            pltpu.VMEM((16, 4, 128), F32),
            pltpu.VMEM((4, 1, 128), F32),
            pltpu.VMEM((8, 1, 128), F32),
            dma((8,)), dma((8,)), dma((2,)), dma((2,)), dma((2, 4)), dma((2, 4)), dma((2, 2)), dma((2, 2)), dma((1,)), dma((1,)),
            dma((2, 8)), dma((2, 8)), dma((2, 8)), dma((2, 8)), dma((4, 8)), dma((4, 8)), dma((3,)),
            dma((16,)), dma((16,)), dma((8,)), dma((8,)),
        ],
        compiler_params=pltpu.CompilerParams(
            collective_id=0, has_side_effects=True, vmem_limit_bytes=VMEM_LIMIT
        ),
    )(inputs.reshape(2, 8 * TOK, ROWS), out_cotangent, sign_bits, row_pick.reshape(64, 128), col_pick.reshape(64, 128))


def solution(mesh):
    return jax.shard_map(
        body,
        mesh=mesh,
        in_specs=(
            P(None, "narrow", "wide"),
            P(None, None, ("wide", "narrow"), None),
            P(None, "wide", "narrow"),
            P(),
            P(),
        ),
        out_specs=P(None, None, ("wide", "narrow")),
        check_vma=False,
    )
```

```python
import functools

import jax
import jax.numpy as jnp
from jax import lax
from jax.experimental import pallas as pl
from jax.experimental.pallas import tpu as pltpu
from jax.sharding import PartitionSpec as P

MESH = pl.DeviceIdType.MESH
F32 = jnp.float32
BF16 = jnp.bfloat16
I32 = jnp.int32
VMEM_LIMIT = 60 << 20

TOK = 32
COLS = 2048
ROWS = 256
SLICES = ((0, 1), (3, 2), (4, 5), (7,), (6,))
MULTIPLY_AT = (7, 9, 11, 12, 12)
LAST = 7


def place():
    wide = lax.axis_index("wide")
    narrow = lax.axis_index("narrow")
    return wide, narrow, wide // 8, (wide // 2) % 4, wide % 2, narrow // 4, narrow % 4


def device(y_hi, z, core, y_lo, x):
    return (y_hi * 8 + z * 2 + core, y_lo * 4 + x)


def remote(src, dst, send, recv, target):
    return pltpu.make_async_remote_copy(
        src_ref=src, dst_ref=dst, send_sem=send, recv_sem=recv, device_id=target, device_id_type=MESH
    )


def fold_parity(value, top):
    while top:
        value = value ^ (value >> top)
        top //= 2
    return value & 1


def hadamard(length):
    rows = lax.broadcasted_iota(I32, (length, length), 0)
    cols = lax.broadcasted_iota(I32, (length, length), 1)
    return (1 - 2 * fold_parity(rows & cols, 8)).astype(F32).astype(BF16)


def split(value):
    high = value.astype(BF16)
    return high, (value - high.astype(F32)).astype(BF16)


def kernel(
    inputs, cot_ref, bits_ref, row_ref, col_ref, out_ref,
    gbuf, xbuf, xt, bits, own_sign, far_sign, acc, table, rows, dot_sign, index_vmem, index, scale,
    terms, first, partial, second,
    a_send, a_recv, y_send, y_recv, x_send, x_recv, h_send, h_recv, s_send, s_recv,
    b_send, b_recv, r_send, r_recv, c_send, c_recv, local_sem, w_send, w_recv, n_send, n_recv,
):
    wide, narrow, y_hi, z, core, y_lo, x = place()
    real = narrow != LAST

    def dev(y_hi=y_hi, z=z, core=core, y_lo=y_lo, x=x):
        return device(y_hi, z, core, y_lo, x)

    z_up, z_down, z_far = (z + 1) % 4, (z + 3) % 4, (z + 2) % 4
    barrier = pltpu.get_barrier_semaphore()
    peers = [(wide, narrow ^ offset) for offset in range(1, 8)]
    peers += [(wide ^ offset, narrow) for offset in range(1, 16)]
    peers += [dev(y_hi=1 - y_hi, y_lo=1 - y_lo)]
    for peer in peers:
        pl.semaphore_signal(barrier, inc=1, device_id=peer, device_id_type=MESH)

    def slot(z_at, core_at, offset):
        return gbuf.at[z_at * 2 + core_at, pl.ds(pl.multiple_of((narrow ^ offset) * TOK, TOK), TOK)]

    def half_slot(direction, z_at, offset):
        base = (narrow ^ offset) * TOK + direction * (TOK // 2)
        return gbuf.at[z_at * 2 + core, pl.ds(pl.multiple_of(base, TOK // 2), TOK // 2)]

    def columns(at):
        return pl.ds(pl.multiple_of(at * COLS, COLS), COLS)

    own_slice = cot_ref.at[0, 0, :, columns(narrow)]
    bits_copy = pltpu.make_async_copy(bits_ref.at[0], bits, local_sem.at[0])
    own_copy = pltpu.make_async_copy(own_slice, slot(z, core, 0), local_sem.at[1])
    index_copy = pltpu.make_async_copy(index_vmem, index, local_sem.at[2])
    bits_copy.start()

    @pl.when(real)
    def _():
        own_copy.start()

    row, col = row_ref[...], col_ref[...]
    index_vmem[...] = (col // 128) % 16 * 512 + row // 2048 * 256 + row % 256
    odd = fold_parity((wide & (row // 256)) ^ (narrow & (col // 2048)), 8)
    scale[...] = jnp.where(odd == 1, F32(-1.0), F32(1.0)) / jnp.sqrt(F32(8192))

    def ring_copy(direction, offset):
        landing = slot(z, core, offset)
        return remote(
            own_slice if offset == 0 else landing, landing,
            b_send.at[direction, offset], b_recv.at[direction, offset],
            dev(z=z_up if direction == 0 else z_down),
        )

    def relay_copy(direction, offset):
        span = half_slot(direction, z_down if direction == 0 else z_up, offset)
        return remote(
            span, span, r_send.at[direction, offset], r_recv.at[direction, offset],
            dev(z=z_up if direction == 0 else z_down),
        )

    z_of = (z, z_down, z_far, z_up)

    def core_copy(distance, offset):
        landing = slot(z_of[distance], core, offset)
        return remote(
            own_slice if distance == 0 and offset == 0 else landing, landing,
            c_send.at[distance, offset], c_recv.at[distance, offset], dev(core=1 - core),
        )

    def pass_on(offset):
        ring_copy(0, offset).start()
        ring_copy(1, offset).start()
        core_copy(0, offset).start()

    pl.semaphore_wait(barrier, len(peers))

    @pl.when(real)
    def _():
        pass_on(0)

    def y_copy(target_lo):
        rel = y_hi ^ y_lo
        return remote(
            inputs, xbuf.at[x, rel], y_send.at[target_lo], y_recv.at[rel],
            dev(y_hi=y_lo, y_lo=target_lo),
        )

    self_copy = pltpu.make_async_copy(inputs, xbuf.at[x, 0], y_recv.at[0])
    for target_lo in range(2):
        mine = (y_hi == y_lo) & (y_lo == target_lo)

        @pl.when(mine)
        def _():
            self_copy.start()

        @pl.when(jnp.logical_not(mine))
        def _():
            y_copy(target_lo).start()

    def a_copy(offset):
        target = narrow ^ offset
        return remote(
            cot_ref.at[0, 0, :, columns(target)],
            slot(z, core, 0),
            a_send.at[offset], a_recv.at[offset],
            dev(y_lo=target // 4, x=target % 4),
        )

    order = (0, 1, 3, 2, 4, 5, 7, 6)

    def send_cotangents(offsets):
        for offset in offsets:

            @pl.when((narrow ^ offset) != LAST)
            def _():
                a_copy(offset).start()

    send_cotangents(order[1:5])

    index_copy.start()

    bits_copy.wait()

    @pl.loop(0, ROWS // 16)
    def _(step):
        span = pl.ds(pl.multiple_of(step * 16, 16), 16)
        own_sign[span, :] = (2 * bits[span, :] - 1).astype(F32).astype(BF16)

    sign_copy = remote(own_sign, far_sign, s_send.at[0], s_recv.at[0], dev(y_hi=1 - y_hi))

    def x_copy(rel, offset):
        block = xbuf.at[x, rel]
        return remote(block, block, x_send.at[rel, offset], x_recv.at[rel, offset], dev(x=x ^ offset))

    def x_relay(rel, half):
        block = xbuf.at[x ^ (1 + 2 * half), rel, half]
        return remote(block, block, h_send.at[rel, half], h_recv.at[rel, half], dev(x=x ^ (3 - 2 * half)))

    def spread_inputs(rel):
        if rel == 0:
            @pl.when(y_hi == y_lo)
            def _():
                self_copy.wait()

            @pl.when(y_hi != y_lo)
            def _():
                remote(inputs, xbuf.at[x, 0], y_send.at[0], y_recv.at[0], dev(y_lo=1 - y_lo)).wait_recv()
        else:
            remote(inputs, xbuf.at[x, 1], y_send.at[0], y_recv.at[1], dev(y_lo=1 - y_lo)).wait_recv()
        for offset in (1, 3):
            x_copy(rel, offset).start()

    def relay_inputs(rel):
        for half in range(2):
            block = xbuf.at[x ^ (1 + 2 * half), rel]
            remote(
                block, block, x_send.at[rel, 1], x_recv.at[rel, 1 + 2 * half], dev(x=x ^ 1)
            ).wait_recv()
            x_relay(rel, half).start()

    def await_inputs():
        for rel in range(2):
            for half in range(2):
                block = xbuf.at[x ^ 2, rel, half]
                remote(block, block, h_send.at[rel, half], h_recv.at[rel, half], dev(x=x ^ 1)).wait_recv()

    lanes = lax.broadcasted_iota(I32, (128, 128), 1)

    def dot_signs(piece):
        for line in range(4 * piece, 4 * piece + 4):
            low = jnp.broadcast_to(col_ref[line:line + 1, :] % 128, (128, 128)).T
            dot_sign[line * 128:line * 128 + 128, :] = (1 - 2 * fold_parity(low & lanes, 4)).astype(F32).astype(BF16)

    def multiply(offsets):
        for distance in range(4):
            for offset in offsets:
                core_copy(distance, offset).wait_recv()
        size = len(offsets) * TOK
        tokens = pl.ds(pl.multiple_of((narrow ^ offsets[0]) // len(offsets) * size, size), size)
        depth = 8 * size
        for rel in range(2):
            xt[rel * ROWS:(rel + 1) * ROWS, :depth] = xbuf[:, rel, :, tokens, :].reshape(depth, ROWS).T

        @pl.loop(0, COLS // 256)
        def _(tile):
            cols = pl.ds(pl.multiple_of(tile * 256, 256), 256)
            part = jnp.dot(xt[:, :depth], gbuf[:, tokens, cols].reshape(depth, 256), preferred_element_type=F32)
            for rel in range(2):
                value = part[rel * ROWS:(rel + 1) * ROWS]
                if 0 not in offsets:
                    value = value + acc[rel, :, cols]
                acc[rel, :, cols] = value

    def wide_copy(offset):
        return remote(
            terms.at[wide ^ offset], first.at[offset], w_send.at[offset], w_recv.at[offset], (wide ^ offset, narrow)
        )

    def mix_rows(mix, rel, sign, cols):
        both = jnp.concatenate(split(acc[rel, :, cols] * sign[:, cols].astype(F32)), axis=0)
        return jnp.dot(mix, both, preferred_element_type=F32)

    @pl.when(real)
    def _():
        sign_copy.start()
        for step in range(1, 13):
            if step < 8:
                remote(
                    own_slice, slot(z, core, order[step]), a_send.at[order[step]], a_recv.at[order[step]],
                    dev(core=1 - core),
                ).wait_recv()
                pass_on(order[step])
            if step in (2, 3):
                spread_inputs(step - 2)
                send_cotangents(order[5:6] if step == 2 else order[6:])
            if step in (4, 5):
                relay_inputs(step - 4)
            if 0 <= step - 2 < 8:
                offset = order[step - 2]
                for direction in range(2):
                    landing = slot(z_down if direction == 0 else z_up, core, offset)
                    remote(
                        landing, landing, b_send.at[direction, offset], b_recv.at[direction, offset], dev(z=z_up)
                    ).wait_recv()
                    relay_copy(direction, offset).start()
                    core_copy(1 if direction == 0 else 3, offset).start()
            if 0 <= step - 5 < 8:
                offset = order[step - 5]
                for direction in range(2):
                    span = half_slot(direction, z_far, offset)
                    remote(
                        span, span, r_send.at[direction, offset], r_recv.at[direction, offset], dev(z=z_up)
                    ).wait_recv()
                core_copy(2, offset).start()
            if step <= 8:
                dot_signs(2 * step - 2)
                dot_signs(2 * step - 1)
            if step == MULTIPLY_AT[0]:
                own_copy.wait()
                await_inputs()
            for at, offsets in zip(MULTIPLY_AT, SLICES, strict=True):
                if step == at:
                    multiply(offsets)

        mix = jnp.concatenate([hadamard(ROWS)] * 2, axis=1)

        @pl.loop(0, 8)
        def _(tile):
            cols = pl.ds(pl.multiple_of(tile * 256, 256), 256)
            acc[0, :, cols] = mix_rows(mix, 0, own_sign, cols)

        sign_copy.wait_recv()

        @pl.loop(0, 8)
        def _(tile):
            cols = pl.ds(pl.multiple_of(tile * 256, 256), 256)
            near, far = acc[0, :, cols], mix_rows(mix, 1, far_sign, cols)
            for rel, value in ((0, near + far), (1, near - far)):
                left, right = value[:, :128], value[:, 128:]
                base = pl.multiple_of(tile * 1024 + rel * ROWS, ROWS)
                table[pl.ds(base, ROWS), :] = left + right
                table[pl.ds(base + 512, ROWS), :] = left - right

        @pl.loop(0, 64)
        def _(step):
            start = pl.multiple_of(step * 8, 8)
            for half in range(2):
                value = [table[pl.ds((2 * tile + half) * 512 + start, 8), :] for tile in range(8)]
                for bit in (1, 2, 4):
                    value = [
                        value[tile ^ bit] - value[tile] if tile & bit else value[tile] + value[tile | bit]
                        for tile in range(8)
                    ]
                for tile in range(8):
                    table[pl.ds((2 * tile + half) * 512 + start, 8), :] = value[tile]

        index_copy.wait()
        rows[1] = jnp.zeros((512, 128), F32)

        def dot_rows(block, held):
            span = pl.ds(pl.multiple_of(block * 512, 512), 512)
            total = jnp.sum((held[...] * dot_sign[span, :].astype(F32)).T, axis=0, keepdims=True)
            for part in range(4):
                terms[block, part:part + 1, :] = (
                    total[:, part * 128:(part + 1) * 128] * scale[pl.ds(block * 4 + part, 1), :]
                )

        def load_rows(block, half):
            for part in range(4):
                for i in range(128):
                    at = part * 128 + i
                    rows[half, at:at + 1, :] = table[pl.ds(index[block * 4 + part, i], 1), :]

        @pl.loop(0, 8)
        def _(step):
            first_block, second_block = wide ^ (15 - 2 * step), wide ^ (14 - 2 * step)
            dot_rows(wide ^ lax.rem(16 - 2 * step, 16), rows.at[1])
            load_rows(first_block, 0)

            @pl.when(step > 0)
            def _():
                wide_copy(16 - 2 * step).start()

            dot_rows(first_block, rows.at[0])
            load_rows(second_block, 1)
            wide_copy(15 - 2 * step).start()

        dot_rows(wide, rows.at[1])

    @pl.when(jnp.logical_not(real))
    def _():
        index_copy.wait()
        terms[...] = jnp.zeros_like(terms)

        @pl.loop(1, 16)
        def _(step):
            wide_copy(16 - step).start()

        for rel in range(2):
            spread_inputs(rel)
            send_cotangents(order[5:6] if rel == 0 else order[6:])
        for rel in range(2):
            relay_inputs(rel)
        await_inputs()

    def narrow_copy(offset):
        target = narrow ^ offset
        return remote(
            partial.at[target // 2], second.at[offset], n_send.at[offset], n_recv.at[offset], (wide, target)
        )

    total = terms[wide]
    for offset in range(15, 0, -1):
        wide_copy(offset).wait_recv()
        total = total + first[offset]
    for line in range(4):
        partial[line] = total[line:line + 1]
    for offset in range(1, 8):
        narrow_copy(offset).start()
    line = partial[narrow // 2]
    for offset in range(1, 8):
        narrow_copy(offset).wait_recv()
        line = line + second[offset]
    out_ref[0] = jnp.where(narrow % 2 == 1, line[:, 64:], line[:, :64])

    @pl.when(real)
    def _():
        sign_copy.wait_send()
        for offset in order:
            for direction in range(2):
                ring_copy(direction, offset).wait_send()
                relay_copy(direction, offset).wait_send()
            for distance in range(4):
                core_copy(distance, offset).wait_send()

    for rel in range(2):
        for half in range(2):
            x_copy(rel, 1 + 2 * half).wait_send()
            x_relay(rel, half).wait_send()
    for target_lo in range(2):
        mine = (y_hi == y_lo) & (y_lo == target_lo)

        @pl.when(jnp.logical_not(mine))
        def _():
            y_copy(target_lo).wait_send()

    for offset in range(1, 8):

        @pl.when((narrow ^ offset) != LAST)
        def _():
            a_copy(offset).wait_send()

    for offset in range(1, 16):
        wide_copy(offset).wait_send()
    for offset in range(1, 8):
        narrow_copy(offset).wait_send()


def body(inputs, out_cotangent, sign_bits, row_pick, col_pick):
    hbm = pl.BlockSpec(memory_space=pl.ANY)
    vmem = pl.BlockSpec(memory_space=pltpu.VMEM)
    dma = pltpu.SemaphoreType.DMA
    return pl.pallas_call(
        kernel,
        out_shape=jax.ShapeDtypeStruct((1, 1, 64), F32),
        in_specs=[hbm, hbm, hbm, vmem, vmem],
        out_specs=vmem,
        scratch_shapes=[
            pltpu.VMEM((8, 8 * TOK, COLS), BF16),
            pltpu.VMEM((4, 2, 2, 8 * TOK, ROWS), BF16),
            pltpu.VMEM((2 * ROWS, 512), BF16),
            pltpu.VMEM((ROWS, COLS), I32),
            pltpu.VMEM((ROWS, COLS), BF16),
            pltpu.VMEM((ROWS, COLS), BF16),
            pltpu.VMEM((2, ROWS, COLS), F32),
            pltpu.VMEM((8192, 128), F32),
            pltpu.VMEM((2, 512, 128), F32),
            pltpu.VMEM((8192, 128), BF16),
            pltpu.VMEM((64, 128), I32),
            pltpu.SMEM((64, 128), I32),
            pltpu.VMEM((64, 128), F32),
            pltpu.VMEM((16, 4, 128), F32),
            pltpu.VMEM((16, 4, 128), F32),
            pltpu.VMEM((4, 1, 128), F32),
            pltpu.VMEM((8, 1, 128), F32),
            dma((8,)), dma((8,)), dma((2,)), dma((2,)), dma((2, 4)), dma((2, 4)), dma((2, 2)), dma((2, 2)), dma((1,)), dma((1,)),
            dma((2, 8)), dma((2, 8)), dma((2, 8)), dma((2, 8)), dma((4, 8)), dma((4, 8)), dma((3,)),
            dma((16,)), dma((16,)), dma((8,)), dma((8,)),
        ],
        compiler_params=pltpu.CompilerParams(
            collective_id=0, has_side_effects=True, vmem_limit_bytes=VMEM_LIMIT
        ),
    )(inputs.reshape(2, 8 * TOK, ROWS), out_cotangent, sign_bits, row_pick.reshape(64, 128), col_pick.reshape(64, 128))


def solution(mesh):
    return jax.shard_map(
        body,
        mesh=mesh,
        in_specs=(
            P(None, "narrow", "wide"),
            P(None, None, ("wide", "narrow"), None),
            P(None, "wide", "narrow"),
            P(),
            P(),
        ),
        out_specs=P(None, None, ("wide", "narrow")),
        check_vma=False,
    )
```
